32 devices in a mesh: row: 4 (over y, core), col: 8 (over z, x).
Axes of the slice: x: 2, y: 2, z: 4, core: 2. Of those that a mesh axis runs over, the one named last changes fastest.
Arguments:
- shell_velocity: bfloat16 [256, 128, 128], P(('row', 'col')), may hold values from -6 to 6
- coupling: bfloat16 [256, 2, 2, 256, 128], P(('row', 'col')), may hold values from -0.375 to 0.375
- coupling_dest: int32 [256, 2], P(('row', 'col')), may hold values from 0 to 7, all different within a row; in each aligned block of 8 rows (0 to 7, 8 to 15, ...) at most 2 rows name the same one
- coupling_cluster: int32 [256, 2], P(('row', 'col')), may hold values from 0 to 63
- near_blocks: bfloat16 [4, 8, 32, 2, 256, 256], P('row', 'col'), may hold values from -0.0625 to 0.0625
- far_v: bfloat16 [4, 8, 64, 2, 32, 256], P('row', 'col'), may hold values from -0.25 to 0.25
- far_u: bfloat16 [4, 8, 64, 2, 32, 256], P('row', 'col'), may hold values from -0.125 to 0.125
- block_pairs: int32 [4, 8, 96], P('row', 'col'), may hold values from 0 to 1023, as said below
Outputs:
- response: bfloat16 [16384, 128], P(('row', 'col'))
The draws below stay inside these ranges and needn't reach their ends.
Inputs may be any that keep to these rules, and one draw needn't show every extreme that they name: `coupling_dest`: the rows of one device name any column group at most 2 times, and some device names one exactly 2 times; the 2 entries of a row differ. `block_pairs`: each entry codes a row cluster r and column cluster c of its group as r * 64 + c; the entries of one group are distinct.
All inputs are finite; a program needn't handle non-finite values.
Results may differ from the reference program's by a relative error of at most 0.008.
Values may be sent and summed in bfloat16 or wider, within the bound.
A program may use at most 128 MiB of HBM per device.

```python
import math
import jax
import jax.numpy as jnp
import numpy as np
from jax import lax

B = 256
RANK = 32
LOAD_CASES = 64
SB = 128
TOP = 2
RC_DEV = 16
CC_DEV = 64
NEAR_DEV = 32
FAR_DEV = 64
SHELL_DEV = 8
ROW_GROUPS = 4
COL_GROUPS = 8
MOST = 2
SHELLS = 256
ROWS = 16384


def draw_block_pairs(key, part):
    keys = jax.random.split(jax.random.fold_in(key, 17), ROW_GROUPS * COL_GROUPS)

    def one_group(group_key):
        return jax.random.permutation(group_key, RC_DEV * CC_DEV)[:NEAR_DEV + FAR_DEV]
    values = jax.vmap(one_group)(keys)
    return values.reshape(ROW_GROUPS, COL_GROUPS, NEAR_DEV + FAR_DEV).astype(jnp.int32)


def with_ends(values, key, smallest, top_value):
    extent = values.shape
    place = [jax.random.randint(jax.random.fold_in(key, axis), (), 0, extent[axis]) for axis in range(len(extent))]
    values = values.at[tuple(place)].set(smallest)
    longest = extent.index(max(extent))
    place[longest] = (place[longest] + 1) % extent[longest]
    return values.at[tuple(place)].set(top_value)


def block_scale(rng, shape, cuts, smallest, high):
    loudness, own = 1.0, jax.random.fold_in(rng, 6)
    for dim, shards_of in cuts:
        draws = jnp.exp(jax.random.uniform(jax.random.fold_in(own, dim), (shards_of,), jnp.float32, smallest / len(cuts), high / len(cuts)))
        loudness = loudness * jnp.repeat(draws, shape[dim] // shards_of).reshape([-1 if axis == dim else 1 for axis in range(len(shape))])
    return loudness


def deal_out(key, own, number, rows, amount, top, bound, lean):
    sequence = jax.random.permutation(key, amount)
    packed, ordinary = portions_of(amount, rows * top, bound, lean, True), portions_of(amount, rows * top, bound, lean, False)
    places = jnp.arange(amount)

    def named(sizes, turn):
        used = int((sizes > 0).sum())
        fixed = max(1, used // 4)
        moved = fixed + (places - fixed + turn * (used - fixed)) % max(1, amount - fixed)
        return jnp.zeros((amount,), jnp.int32).at[sequence[jnp.where(places < fixed, places, moved)]].set(jnp.asarray(sizes, jnp.int32))

    sizes = jnp.where(number % 4 == 0, named(packed, number // 4), named(ordinary, number - number // 4 - 1))
    mixed = jax.random.permutation(jax.random.fold_in(own, 3), amount)
    source_of, sink = mixed[0:amount // 2 * 2:2], mixed[1:amount // 2 * 2:2]
    margin = jnp.minimum(sizes[source_of] - 1, bound - sizes[sink]) // 2
    margin = jnp.where((source_of == sequence[0]) | (sink == sequence[0]) | (sizes[sink] == 0), 0, jnp.maximum(margin, 0))
    moved = jax.random.randint(jax.random.fold_in(own, 4), (amount // 2,), 0, 1 << 20) % (margin + 1)
    sizes = sizes.at[source_of].add(-moved).at[sink].add(moved)
    members = jnp.searchsorted(jnp.cumsum(sizes), jnp.arange(rows * top), side="right").astype(jnp.int32)
    grid = members.reshape(top, rows).T
    grid = grid[jax.random.permutation(jax.random.fold_in(own, 1), rows)]
    turn = jax.random.randint(jax.random.fold_in(own, 2), (rows, 1), 0, top)
    return jnp.take_along_axis(grid, (jnp.arange(top)[None, :] + turn) % top, axis=1)


def portions_of(amount, total, limit, skew, full):
    loads = [(1 << 20) // math.isqrt(standing ** skew) + 1 for standing in range(1, amount + 1)]
    largest = limit if full else min(limit, max(-(-total // amount), total * loads[0] // sum(loads)))
    least = 1 if total - largest >= amount - 1 else 0
    counts, surplus = [largest] + [least] * (amount - 1), total - largest - least * (amount - 1)
    while surplus > 0:
        free = [i for i in range(1, amount) if counts[i] < largest] or [i for i in range(1, amount) if counts[i] < limit]
        pool, budget = sum([loads[i] for i in free]), surplus
        for i in free:
            addition = min(limit - counts[i], max(1, budget * loads[i] // pool), surplus)
            counts[i] = counts[i] + addition
            surplus = surplus - addition
    return np.array(counts)


def scatter_about(key, shape, deviation, limit, shards=(), kind=jnp.bfloat16):
    entries = deviation * jax.random.normal(key, shape, jnp.float32)
    if shards:
        entries = entries * block_scale(key, shape, shards, -0.22, 0.18)
    return jnp.clip(entries, -limit, limit).astype(kind)


def setup_inputs(seed: int = 0) -> dict:
    key_of = jax.random.split(jax.random.key(seed), 9)
    shell_velocity = scatter_about(key_of[0], (SHELLS, SB, 2 * LOAD_CASES), 1.0, 6.0, ((0, 32),))
    coupling = scatter_about(key_of[1], (SHELLS, TOP, 2, B, SB), (2 * SB) ** -0.5, 0.375, ((0, 32),))
    coupling_dest_keys = jax.random.split(jax.random.fold_in(key_of[2], 1), SHELLS // SHELL_DEV)
    coupling_dest_turns = jax.random.permutation(jax.random.fold_in(key_of[2], 3), SHELLS // SHELL_DEV)
    coupling_dest = jax.vmap(lambda own, number: deal_out(jax.random.fold_in(key_of[2], 2), own, number, SHELL_DEV, COL_GROUPS, TOP, MOST, 2))(coupling_dest_keys, coupling_dest_turns).reshape((SHELLS, TOP))
    coupling_cluster = with_ends(jax.random.randint(key_of[3], (SHELLS, TOP), 0, CC_DEV), jax.random.fold_in(key_of[3], 1), 0, CC_DEV - 1).astype(jnp.int32)
    near_blocks = scatter_about(key_of[4], (ROW_GROUPS, COL_GROUPS, NEAR_DEV, 2, B, B), (2 * B * COL_GROUPS * NEAR_DEV // RC_DEV) ** -0.5, 0.0625, ((0, 4), (1, 8)))
    far_v = scatter_about(key_of[5], (ROW_GROUPS, COL_GROUPS, FAR_DEV, 2, RANK, B), (2 * B) ** -0.5, 0.25, ((0, 4), (1, 8)))
    far_u = scatter_about(key_of[6], (ROW_GROUPS, COL_GROUPS, FAR_DEV, 2, RANK, B), (2 * RANK * COL_GROUPS * FAR_DEV // RC_DEV) ** -0.5, 0.125, ((0, 4), (1, 8)))
    block_pairs = draw_block_pairs(jax.random.fold_in(key_of[8], 71), 0)
    return {"shell_velocity": shell_velocity, "coupling": coupling, "coupling_dest": coupling_dest, "coupling_cluster": coupling_cluster, "near_blocks": near_blocks, "far_v": far_v, "far_u": far_u, "block_pairs": block_pairs}


def rotate_blocks(values, load_count):
    return jnp.concatenate([-values[..., load_count:], values[..., :load_count]], axis=-1)


def reference(shell_velocity, coupling, coupling_dest, coupling_cluster, near_blocks, far_v, far_u, block_pairs):
    width = 2 * LOAD_CASES

    def shell_terms(inputs):
        coup, velo = inputs
        coup_f = coup.astype(jnp.float32)
        velo_f = velo.astype(jnp.float32)
        out = jnp.einsum('stpq,sqk->stpk', coup_f[:, :, 0], velo_f)
        out = out + jnp.einsum('stpq,sqk->stpk', coup_f[:, :, 1], rotate_blocks(velo_f, LOAD_CASES))
        return out.astype(jnp.bfloat16)

    groups = SHELLS // SHELL_DEV
    contributions = lax.map(shell_terms, (coupling.reshape(groups, SHELL_DEV, TOP, 2, B, SB),
                                          shell_velocity.reshape(groups, SHELL_DEV, SB, width)))
    contributions = lax.optimization_barrier(contributions.reshape(SHELLS * TOP, B, width))
    target = (coupling_dest * CC_DEV + coupling_cluster).reshape(-1).astype(jnp.int32)
    source_sum = jax.ops.segment_sum(contributions.astype(jnp.float32), target, num_segments=COL_GROUPS * CC_DEV)
    sources = source_sum.astype(jnp.bfloat16).reshape(COL_GROUPS, CC_DEV, B, width)

    def group_terms(inputs):
        near_group, right_group, left_group, pair_group, col_group = inputs
        local_src = lax.optimization_barrier(sources[col_group]).astype(jnp.float32)
        owners = (pair_group // CC_DEV).astype(jnp.int32)
        columns = (pair_group % CC_DEV).astype(jnp.int32)
        nearby_input = local_src[columns[:NEAR_DEV]]
        nearby_factor = near_group.astype(jnp.float32)
        nearby_contribution = jnp.einsum('dym,dmg->dyg', nearby_factor[:, 0], nearby_input)
        nearby_contribution = nearby_contribution + jnp.einsum('dym,dmg->dyg', nearby_factor[:, 1], rotate_blocks(nearby_input, LOAD_CASES))
        distant_input = local_src[columns[NEAR_DEV:]]
        right_factor_matrix = right_group.astype(jnp.float32)
        expansion_coefficients = jnp.einsum('dyz,dzi->dyi', right_factor_matrix[:, 0], distant_input)
        expansion_coefficients = expansion_coefficients + jnp.einsum('dyz,dzi->dyi', right_factor_matrix[:, 1], rotate_blocks(distant_input, LOAD_CASES))
        expansion_coefficients = lax.optimization_barrier(expansion_coefficients.astype(jnp.bfloat16)).astype(jnp.float32)
        left_f = left_group.astype(jnp.float32)
        far_term = jnp.einsum('brp,brk->bpk', left_f[:, 0], expansion_coefficients)
        far_term = far_term + jnp.einsum('brp,brk->bpk', left_f[:, 1], rotate_blocks(expansion_coefficients, LOAD_CASES))
        all_terms = jnp.concatenate([nearby_contribution, far_term], axis=0)
        return jax.ops.segment_sum(all_terms, owners, num_segments=RC_DEV)

    count = ROW_GROUPS * COL_GROUPS
    col_index = (jnp.arange(count) % COL_GROUPS).astype(jnp.int32)
    partials = lax.map(group_terms, (
        near_blocks.reshape(count, NEAR_DEV, 2, B, B),
        far_v.reshape(count, FAR_DEV, 2, RANK, B),
        far_u.reshape(count, FAR_DEV, 2, RANK, B),
        block_pairs.reshape(count, NEAR_DEV + FAR_DEV),
        col_index))
    partials = partials.reshape(ROW_GROUPS, COL_GROUPS, RC_DEV * B, width)
    response = jnp.sum(partials, axis=1).astype(jnp.bfloat16)
    return response.reshape(ROWS, width)
```

```python
import functools

import jax
import jax.numpy as jnp
from jax import lax
from jax.experimental import pallas as pl
from jax.experimental.pallas import tpu as pltpu
from jax.sharding import PartitionSpec as P

RC_DEV = 16
CC_DEV = 64
NEAR_DEV = 32
CORES = 2
TAIL = 16
MESH = pl.DeviceIdType.MESH


def rotate(values):
    half = values.shape[-1] // 2
    lane = lax.broadcasted_iota(jnp.int32, values.shape, values.ndim - 1)
    turned = pltpu.roll(values, half, values.ndim - 1)
    return jnp.where(lane < half, -turned, turned)


def flip(index, mask, size):
    result, bit = 0, 1
    while bit < size:
        result = result + bit * ((index // bit + mask // bit) % 2)
        bit *= 2
    return result


def exchange_kernel(
    rows, cols, capacity, dest_ref, cluster_ref, coupling_ref, velocity_ref, got_ref,
    outgoing, send_col, send_y, send_core, recv,
):
    g, h = lax.axis_index("row"), lax.axis_index("col")
    entries, twice, _ = coupling_ref.shape
    panels = twice // 2
    top = entries // velocity_ref.shape[0]
    peers = rows // CORES
    y, core = g // CORES, g % CORES
    mate = y * CORES + (CORES - 1 - core)

    barrier = pltpu.get_barrier_semaphore()
    for step in range(1, cols):
        pl.semaphore_signal(barrier, inc=1, device_id=(g, (h + step) % cols), device_id_type=MESH)
    for step in range(1, peers):
        pl.semaphore_signal(
            barrier, inc=1, device_id=((y + step) % peers * CORES + core, h), device_id_type=MESH
        )
    pl.semaphore_signal(barrier, inc=1, device_id=(mate, h), device_id_type=MESH)

    def fill(dst, target):
        picked = [jnp.int32(-1)] * capacity
        count = jnp.int32(0)
        for e in range(entries):
            hit = dest_ref[e] == target
            for k in range(capacity):
                picked[k] = jnp.where(hit & (count == k), e, picked[k])
            count = count + jnp.where(hit, 1, 0)
        for k in range(capacity):
            valid = picked[k] >= 0
            e = jnp.maximum(picked[k], 0)
            product = jnp.dot(
                coupling_ref[e], velocity_ref[e // top], preferred_element_type=jnp.float32
            )
            value = product[:panels] + rotate(product[panels:])
            scale = jnp.where(valid, 1.0, 0.0)
            dst[k, pl.ds(0, panels), :] = (value * scale).astype(jnp.bfloat16)
            number = jnp.where(valid, cluster_ref[e], 0).astype(jnp.float32)
            dst[k, pl.ds(panels, TAIL), :] = jnp.full(
                (TAIL, value.shape[-1]), number, jnp.float32
            ).astype(jnp.bfloat16)

    def col_copy(j):
        target = flip(h, j, cols)
        return pltpu.make_async_remote_copy(
            src_ref=outgoing.at[j],
            dst_ref=got_ref.at[g, h],
            send_sem=send_col.at[j],
            recv_sem=recv.at[g, h],
            device_id=(g, target),
            device_id_type=MESH,
        )

    def y_copy(step, j):
        source = flip(h, j, cols)
        return pltpu.make_async_remote_copy(
            src_ref=got_ref.at[g, source],
            dst_ref=got_ref.at[g, source],
            send_sem=send_y.at[step, j],
            recv_sem=recv.at[g, source],
            device_id=((y + step) % peers * CORES + core, h),
            device_id_type=MESH,
        )

    def core_copy(step, j):
        source = flip(h, j, cols)
        origin = (y + step) % peers * CORES + core
        return pltpu.make_async_remote_copy(
            src_ref=got_ref.at[origin, source],
            dst_ref=got_ref.at[origin, source],
            send_sem=send_core.at[step, j],
            recv_sem=recv.at[origin, source],
            device_id=(mate, h),
            device_id_type=MESH,
        )

    def arrived(origin, j):
        source = flip(h, j, cols)
        pltpu.make_async_copy(
            got_ref.at[origin, source], got_ref.at[origin, source], recv.at[origin, source]
        ).wait()

    fill(got_ref.at[g, h], h)
    pl.semaphore_wait(barrier, cols - 1 + peers - 1 + 1)
    for step in range(1, peers):
        y_copy(step, 0).start()
    core_copy(0, 0).start()

    @pl.loop(1, cols)
    def _(j):
        fill(outgoing.at[j], flip(h, j, cols))
        col_copy(j).start()

    lag = cols // 2

    def relay(j):
        for step in range(1, peers):
            arrived((y + step) % peers * CORES + core, j)
            core_copy(step, j).start()

    @pl.loop(1, lag)
    def _(j):
        arrived(g, j)
        for step in range(1, peers):
            y_copy(step, j).start()
        core_copy(0, j).start()

    @pl.loop(lag, cols)
    def _(j):
        arrived(g, j)
        for step in range(1, peers):
            y_copy(step, j).start()
        core_copy(0, j).start()
        relay(j - lag)

    @pl.loop(cols - lag, cols)
    def _(j):
        relay(j)

    @pl.loop(0, cols)
    def _(j):
        for step in range(peers):
            arrived((y + step) % peers * CORES + (CORES - 1 - core), j)

    @pl.loop(1, cols)
    def _(j):
        col_copy(j).wait_send()

    @pl.loop(0, cols)
    def _(j):
        for step in range(1, peers):
            y_copy(step, j).wait_send()
        for step in range(peers):
            core_copy(step, j).wait_send()


def field_kernel(
    steps, ids_ref, pairs_ref, got_ref, near_ref, v_ref, u_ref, out_ref,
    head, link, sources, total,
):
    step = pl.program_id(0)
    slots, _, width = got_ref.shape
    near_count, twice, panels = near_ref.shape
    far_count, rank2, _ = v_ref.shape
    rank = rank2 // 2

    @pl.when(step == 0)
    def _():
        @pl.loop(0, CC_DEV)
        def _(c):
            head[c] = -1

        @pl.loop(0, slots)
        def _(n):
            c = ids_ref[n]
            link[n] = head[c]
            head[c] = n

        @pl.loop(0, CC_DEV)
        def _(c):
            def more(state):
                return state[0] >= 0

            def add(state):
                n, value = state
                return link[n], value + got_ref[n, pl.ds(0, panels), :].astype(jnp.float32)

            _, value = lax.while_loop(
                more, add, (head[c], jnp.zeros((panels, width), jnp.float32))
            )
            sources[c] = value.astype(jnp.bfloat16)

        total[...] = jnp.zeros_like(total)

    for b in range(near_count):
        code = pairs_ref[step * near_count + b]
        total[code // CC_DEV] += jnp.dot(
            near_ref[b], sources[code % CC_DEV], preferred_element_type=jnp.float32
        )

    for b in range(far_count):
        code = pairs_ref[steps * near_count + step * far_count + b]
        part = jnp.dot(v_ref[b], sources[code % CC_DEV], preferred_element_type=jnp.float32)
        coeffs = part[:rank] + rotate(part[rank:])
        both = jnp.concatenate([coeffs, rotate(coeffs)], axis=0).astype(jnp.bfloat16)
        total[code // CC_DEV, pl.ds(0, panels), :] += lax.dot_general(
            u_ref[b], both, (((0,), (0,)), ((), ())), preferred_element_type=jnp.float32
        )

    @pl.when(step == steps - 1)
    def _():
        @pl.loop(0, RC_DEV)
        def _(r):
            value = total[r, pl.ds(0, panels), :] + rotate(total[r, pl.ds(panels, panels), :])
            out_ref[r] = value.astype(jnp.bfloat16)


def reduce_kernel(
    zs, xs, part_ref, out_ref, first, middle, second, send1, recv1, send2, recv2
):
    g, h = lax.axis_index("row"), lax.axis_index("col")
    z, x = h // xs, h % xs

    barrier = pltpu.get_barrier_semaphore()
    for d in range(1, xs):
        pl.semaphore_signal(
            barrier, inc=1, device_id=(g, z * xs + (x + d) % xs), device_id_type=MESH
        )
    for k in range(1, zs):
        pl.semaphore_signal(
            barrier, inc=1, device_id=(g, (z + k) % zs * xs + x), device_id_type=MESH
        )
    pl.semaphore_wait(barrier, xs - 1 + zs - 1)

    def x_copy(k, d):
        goal, other = flip(z, k, zs), (x + d) % xs
        return pltpu.make_async_remote_copy(
            src_ref=part_ref.at[goal * xs + other],
            dst_ref=first.at[goal, x],
            send_sem=send1.at[goal, other],
            recv_sem=recv1.at[goal, x],
            device_id=(g, z * xs + other),
            device_id_type=MESH,
        )

    def z_copy(k):
        goal = flip(z, k, zs)
        return pltpu.make_async_remote_copy(
            src_ref=middle.at[goal],
            dst_ref=second.at[z],
            send_sem=send2.at[goal],
            recv_sem=recv2.at[z],
            device_id=(g, goal * xs + x),
            device_id_type=MESH,
        )

    for k in reversed(range(zs)):
        for d in range(1, xs):
            x_copy(k, d).start()
    for k in reversed(range(zs)):
        goal = flip(z, k, zs)
        value = part_ref[goal * xs + x].astype(jnp.float32)
        for d in range(1, xs):
            other = (x + d) % xs
            pltpu.make_async_copy(
                first.at[goal, other], first.at[goal, other], recv1.at[goal, other]
            ).wait()
            value = value + first[goal, other].astype(jnp.float32)
        if k:
            middle[goal] = value.astype(jnp.bfloat16)
            z_copy(k).start()
    for k in range(1, zs):
        source = flip(z, k, zs)
        pltpu.make_async_copy(second.at[source], second.at[source], recv2.at[source]).wait()
        value = value + second[source].astype(jnp.float32)
    out_ref[...] = value.astype(jnp.bfloat16)
    for k in range(zs):
        for d in range(1, xs):
            x_copy(k, d).wait_send()
        if k:
            z_copy(k).wait_send()


def per_device(
    row_count, col_count,
    shell_velocity, coupling, coupling_dest, coupling_cluster, near_blocks, far_v, far_u,
    block_pairs,
):
    width = shell_velocity.shape[-1]
    shells, top, _, panels, depth = coupling.shape
    entries = shells * top
    capacity = max(2, (entries + col_count - 1) // col_count)
    peers = row_count // CORES
    message = (capacity, panels + TAIL, width)
    vmem = pl.BlockSpec(memory_space=pltpu.VMEM)
    smem = pl.BlockSpec(memory_space=pltpu.SMEM)
    dma = pltpu.SemaphoreType.DMA

    got = pl.pallas_call(
        functools.partial(exchange_kernel, row_count, col_count, capacity),
        out_shape=jax.ShapeDtypeStruct((row_count, col_count) + message, jnp.bfloat16),
        in_specs=[smem, smem, vmem, vmem],
        out_specs=vmem,
        scratch_shapes=[
            pltpu.VMEM((col_count,) + message, jnp.bfloat16),
            dma((col_count,)),
            dma((peers, col_count)),
            dma((peers, col_count)),
            dma((row_count, col_count)),
        ],
        compiler_params=pltpu.CompilerParams(
            collective_id=0, has_side_effects=True, vmem_limit_bytes=48 * 1024 * 1024
        ),
        name="exchange",
    )(
        coupling_dest.reshape(entries),
        coupling_cluster.reshape(entries),
        coupling.reshape(entries, 2 * panels, depth),
        shell_velocity,
    )

    slots = row_count * col_count * capacity
    got = got.reshape(slots, panels + TAIL, width)
    ids = got[:, panels, 0].astype(jnp.int32)
    near_count, far_count, rank = near_blocks.shape[2], far_v.shape[2], far_v.shape[4]
    near = near_blocks.reshape(near_count, 2 * panels, panels)
    right = far_v.reshape(far_count, 2 * rank, panels)
    left = far_u.reshape(far_count, 2 * rank, panels)
    steps = 8
    partial_rows = pl.pallas_call(
        functools.partial(field_kernel, steps),
        grid=(steps,),
        out_shape=jax.ShapeDtypeStruct((RC_DEV, panels, width), jnp.bfloat16),
        in_specs=[
            smem,
            smem,
            vmem,
            pl.BlockSpec((near_count // steps, 2 * panels, panels), lambda i: (i, 0, 0)),
            pl.BlockSpec((far_count // steps, 2 * rank, panels), lambda i: (i, 0, 0)),
            pl.BlockSpec((far_count // steps, 2 * rank, panels), lambda i: (i, 0, 0)),
        ],
        out_specs=pl.BlockSpec((RC_DEV, panels, width), lambda i: (0, 0, 0)),
        scratch_shapes=[
            pltpu.SMEM((CC_DEV,), jnp.int32),
            pltpu.SMEM((slots,), jnp.int32),
            pltpu.VMEM((CC_DEV, panels, width), jnp.bfloat16),
            pltpu.VMEM((RC_DEV, 2 * panels, width), jnp.float32),
        ],
        compiler_params=pltpu.CompilerParams(vmem_limit_bytes=56 * 1024 * 1024),
        name="fields",
    )(ids, block_pairs.reshape(-1), got, near, right, left)

    out_rows = RC_DEV * panels // col_count
    xs = 1
    while 4 * xs * xs <= col_count:
        xs *= 2
    zs = col_count // xs
    return pl.pallas_call(
        functools.partial(reduce_kernel, zs, xs),
        out_shape=jax.ShapeDtypeStruct((out_rows, width), jnp.bfloat16),
        in_specs=[vmem],
        out_specs=vmem,
        scratch_shapes=[
            pltpu.VMEM((zs, xs, out_rows, width), jnp.bfloat16),
            pltpu.VMEM((zs, out_rows, width), jnp.bfloat16),
            pltpu.VMEM((zs, out_rows, width), jnp.bfloat16),
            dma((zs, xs)),
            dma((zs, xs)),
            dma((zs,)),
            dma((zs,)),
        ],
        compiler_params=pltpu.CompilerParams(
            collective_id=1, has_side_effects=True, vmem_limit_bytes=32 * 1024 * 1024
        ),
        name="reduce",
    )(partial_rows.reshape(col_count, out_rows, width))


def solution(mesh):
    return jax.shard_map(
        functools.partial(per_device, mesh.shape["row"], mesh.shape["col"]),
        mesh=mesh,
        in_specs=(
            P(("row", "col"), None, None),
            P(("row", "col"), None, None, None, None),
            P(("row", "col"), None),
            P(("row", "col"), None),
            P("row", "col", None, None, None, None),
            P("row", "col", None, None, None, None),
            P("row", "col", None, None, None, None),
            P("row", "col", None),
        ),
        out_specs=P(("row", "col"), None),
        check_vma=False,
    )
```

```python
import functools

import jax
import jax.numpy as jnp
from jax import lax
from jax.experimental import pallas as pl
from jax.experimental.pallas import tpu as pltpu
from jax.sharding import PartitionSpec as P

RC_DEV = 16
CC_DEV = 64
NEAR_DEV = 32
CORES = 2
TAIL = 16
MESH = pl.DeviceIdType.MESH


def rotate(values):
    half = values.shape[-1] // 2
    lane = lax.broadcasted_iota(jnp.int32, values.shape, values.ndim - 1)
    turned = pltpu.roll(values, half, values.ndim - 1)
    return jnp.where(lane < half, -turned, turned)


def flip(index, mask, size):
    result, bit = 0, 1
    while bit < size:
        result = result + bit * ((index // bit + mask // bit) % 2)
        bit *= 2
    return result


def exchange_kernel(
    rows, cols, capacity, dest_ref, cluster_ref, coupling_hbm, velocity_hbm, got_ref, ids_ref,
    coupling_ref, velocity_ref, outgoing, tails, load_sem, tail_sem, send_col, send_y,
    send_core, recv,
):
    g, h = lax.axis_index("row"), lax.axis_index("col")
    entries, twice, _ = coupling_ref.shape
    panels = twice // 2
    width = velocity_ref.shape[-1]
    top = entries // velocity_ref.shape[0]
    peers = rows // CORES
    y, core = g // CORES, g % CORES
    mate = y * CORES + (CORES - 1 - core)

    loads = (
        pltpu.make_async_copy(coupling_hbm, coupling_ref, load_sem.at[0]),
        pltpu.make_async_copy(velocity_hbm, velocity_ref, load_sem.at[1]),
    )
    for load in loads:
        load.start()

    barrier = pltpu.get_barrier_semaphore()
    for step in range(1, cols):
        pl.semaphore_signal(barrier, inc=1, device_id=(g, (h + step) % cols), device_id_type=MESH)
    for step in range(1, peers):
        pl.semaphore_signal(
            barrier, inc=1, device_id=((y + step) % peers * CORES + core, h), device_id_type=MESH
        )
    pl.semaphore_signal(barrier, inc=1, device_id=(mate, h), device_id_type=MESH)
    for load in loads:
        load.wait()

    def fill(j):
        target = flip(h, j, cols)
        picked = [jnp.int32(-1)] * capacity
        count = jnp.int32(0)
        for e in range(entries):
            hit = dest_ref[e // top, e % top] == target
            for k in range(capacity):
                picked[k] = jnp.where(hit & (count == k), e, picked[k])
            count = count + jnp.where(hit, 1, 0)
        lane = lax.broadcasted_iota(jnp.int32, (TAIL, width), 1)
        tail = jnp.zeros((TAIL, width), jnp.float32)
        for k in range(capacity):
            valid = picked[k] >= 0
            e = jnp.maximum(picked[k], 0)
            product = jnp.dot(
                coupling_ref[e], velocity_ref[e // top], preferred_element_type=jnp.float32
            )
            value = product[:panels] + rotate(product[panels:])
            scale = jnp.where(valid, 1.0, 0.0)
            outgoing[j, pl.ds(k * panels, panels), :] = (value * scale).astype(jnp.bfloat16)
            number = jnp.where(valid, cluster_ref[e // top, e % top], 0).astype(jnp.float32)
            tail = jnp.where(lane == k, number, tail)
        outgoing[j, pl.ds(capacity * panels, TAIL), :] = tail.astype(jnp.bfloat16)

    def col_copy(j):
        target = flip(h, j, cols)
        return pltpu.make_async_remote_copy(
            src_ref=outgoing.at[j],
            dst_ref=got_ref.at[g, h],
            send_sem=send_col.at[j],
            recv_sem=recv.at[g, h],
            device_id=(g, target),
            device_id_type=MESH,
        )

    def relay_copy(origin, source, block, send_sem, row):
        return pltpu.make_async_remote_copy(
            src_ref=block,
            dst_ref=got_ref.at[origin, source],
            send_sem=send_sem,
            recv_sem=recv.at[origin, source],
            device_id=(row, h),
            device_id_type=MESH,
        )

    def y_copy(step, j, block=None):
        source = flip(h, j, cols)
        return relay_copy(
            g, source, got_ref.at[g, source] if block is None else block,
            send_y.at[step, j], (y + step) % peers * CORES + core,
        )

    def core_copy(step, j, block=None):
        source = flip(h, j, cols)
        origin = (y + step) % peers * CORES + core
        return relay_copy(
            origin, source, got_ref.at[origin, source] if block is None else block,
            send_core.at[step, j], mate,
        )

    def arrived(origin, j):
        source = flip(h, j, cols)
        pltpu.make_async_copy(
            got_ref.at[origin, source], got_ref.at[origin, source], recv.at[origin, source]
        ).wait()

    fill(0)
    own = pltpu.make_async_copy(outgoing.at[0], got_ref.at[g, h], send_col.at[0])
    own.start()
    pl.semaphore_wait(barrier, cols - 1 + peers - 1 + 1)
    for step in range(1, peers):
        y_copy(step, 0, outgoing.at[0]).start()
    core_copy(0, 0, outgoing.at[0]).start()

    half = cols // 2

    @pl.loop(1, cols)
    def _(i):
        j = (i % 2) * half + i // 2
        fill(j)
        col_copy(j).start()

    lag = cols // 2

    def pass_on(i):
        j = (i % 2) * half + i // 2
        arrived(g, j)
        for step in range(1, peers):
            y_copy(step, j).start()
        core_copy(0, j).start()

    def relay(i):
        j = (i % 2) * half + i // 2
        for step in range(1, peers):
            arrived((y + step) % peers * CORES + core, j)
            core_copy(step, j).start()

    @pl.loop(1, lag)
    def _(i):
        pass_on(i)

    @pl.loop(lag, cols)
    def _(i):
        pass_on(i)
        relay(i - lag)

    @pl.loop(cols - lag, cols)
    def _(i):
        relay(i)

    @pl.loop(0, cols)
    def _(j):
        for step in range(peers):
            arrived((y + step) % peers * CORES + (CORES - 1 - core), j)

    own.wait()
    gather = pltpu.make_async_copy(
        got_ref.at[:, :, pl.ds(capacity * panels, TAIL), :], tails, tail_sem.at[0]
    )
    gather.start()
    gather.wait()
    for q in range(rows * cols):
        row = tails[q // cols, q % cols].astype(jnp.float32)
        ids_ref[pl.ds(q, 1), :] = row[:1].astype(jnp.int32)

    @pl.loop(1, cols)
    def _(j):
        col_copy(j).wait_send()

    for step in range(1, peers):
        y_copy(step, 0, outgoing.at[0]).wait_send()
    core_copy(0, 0, outgoing.at[0]).wait_send()
    for step in range(1, peers):
        core_copy(step, 0).wait_send()

    @pl.loop(1, cols)
    def _(j):
        for step in range(1, peers):
            y_copy(step, j).wait_send()
        for step in range(peers):
            core_copy(step, j).wait_send()


def field_kernel(
    steps, capacity, ids_ref, pairs_ref, got_ref, near_ref, v_ref, u_ref, out_ref,
    head, link, sources, near_total, far_total,
):
    step = pl.program_id(0)
    messages, _, width = got_ref.shape
    near_count, twice, panels = near_ref.shape
    far_count, rank2, _ = v_ref.shape
    rank = rank2 // 2

    @pl.when(step == 0)
    def _():
        @pl.loop(0, CC_DEV)
        def _(c):
            head[c] = -1

        @pl.loop(0, messages)
        def _(q):
            for k in range(capacity):
                c = ids_ref[q, k]
                link[q * capacity + k] = head[c]
                head[c] = q * capacity + k

        @pl.loop(0, CC_DEV)
        def _(c):
            def more(state):
                return state[0] >= 0

            def add(state):
                n, value = state
                start = pl.multiple_of(n % capacity * panels, panels)
                block = got_ref[n // capacity, pl.ds(start, panels), :]
                return link[n], value + block.astype(jnp.float32)

            _, value = lax.while_loop(
                more, add, (head[c], jnp.zeros((panels, width), jnp.float32))
            )
            sources[c] = value.astype(jnp.bfloat16)

        near_total[...] = jnp.zeros_like(near_total)
        far_total[...] = jnp.zeros_like(far_total)

    codes = [pairs_ref[steps * near_count + step * far_count + b] for b in range(far_count)]
    parts = [
        jnp.dot(v_ref[b], sources[codes[b] % CC_DEV], preferred_element_type=jnp.float32)
        for b in range(far_count)
    ]
    boths = []
    for part in parts:
        coeffs = part[:rank] + rotate(part[rank:])
        boths.append(jnp.concatenate([coeffs, rotate(coeffs)], axis=0).astype(jnp.bfloat16))

    for b in range(near_count):
        code = pairs_ref[step * near_count + b]
        near_total[code // CC_DEV] += jnp.dot(
            near_ref[b], sources[code % CC_DEV], preferred_element_type=jnp.float32
        )

    for b in range(far_count):
        far_total[codes[b] // CC_DEV] += lax.dot_general(
            u_ref[b], boths[b], (((0,), (0,)), ((), ())), preferred_element_type=jnp.float32
        )

    @pl.when(step == steps - 1)
    def _():
        @pl.loop(0, RC_DEV)
        def _(r):
            value = near_total[r, pl.ds(0, panels), :] + far_total[r]
            value = value + rotate(near_total[r, pl.ds(panels, panels), :])
            out_ref[r] = value.astype(jnp.bfloat16)


def reduce_kernel(
    zs, xs, part_ref, out_ref, mine, first, middle, second, load_sem, send1, recv1, send2, recv2
):
    g, h = lax.axis_index("row"), lax.axis_index("col")
    z, x = h // xs, h % xs

    loads = [
        pltpu.make_async_copy(part_ref.at[goal * xs + x], mine.at[goal], load_sem.at[goal])
        for goal in range(zs)
    ]
    for load in loads:
        load.start()

    barrier = pltpu.get_barrier_semaphore()
    for d in range(1, xs):
        pl.semaphore_signal(
            barrier, inc=1, device_id=(g, z * xs + (x + d) % xs), device_id_type=MESH
        )
    for k in range(1, zs):
        pl.semaphore_signal(
            barrier, inc=1, device_id=(g, (z + k) % zs * xs + x), device_id_type=MESH
        )
    pl.semaphore_wait(barrier, xs - 1 + zs - 1)

    def x_copy(k, d):
        goal, other = flip(z, k, zs), (x + d) % xs
        return pltpu.make_async_remote_copy(
            src_ref=part_ref.at[goal * xs + other],
            dst_ref=first.at[goal, x],
            send_sem=send1.at[goal, other],
            recv_sem=recv1.at[goal, x],
            device_id=(g, z * xs + other),
            device_id_type=MESH,
        )

    def z_copy(k):
        goal = flip(z, k, zs)
        return pltpu.make_async_remote_copy(
            src_ref=middle.at[goal],
            dst_ref=second.at[z],
            send_sem=send2.at[goal],
            recv_sem=recv2.at[z],
            device_id=(g, goal * xs + x),
            device_id_type=MESH,
        )

    for k in reversed(range(zs)):
        for d in range(1, xs):
            x_copy(k, d).start()
    for load in loads:
        load.wait()
    for k in reversed(range(zs)):
        goal = flip(z, k, zs)
        value = mine[goal].astype(jnp.float32)
        for d in range(1, xs):
            other = (x + d) % xs
            pltpu.make_async_copy(
                first.at[goal, other], first.at[goal, other], recv1.at[goal, other]
            ).wait()
            value = value + first[goal, other].astype(jnp.float32)
        if k:
            middle[goal] = value.astype(jnp.bfloat16)
            z_copy(k).start()
    for k in range(1, zs):
        source = flip(z, k, zs)
        pltpu.make_async_copy(second.at[source], second.at[source], recv2.at[source]).wait()
        value = value + second[source].astype(jnp.float32)
    out_ref[...] = value.astype(jnp.bfloat16)
    for k in range(zs):
        for d in range(1, xs):
            x_copy(k, d).wait_send()
        if k:
            z_copy(k).wait_send()


def per_device(
    row_count, col_count,
    shell_velocity, coupling, coupling_dest, coupling_cluster, near_blocks, far_v, far_u,
    block_pairs,
):
    width = shell_velocity.shape[-1]
    shells, top, _, panels, depth = coupling.shape
    entries = shells * top
    capacity = max(2, (entries + col_count - 1) // col_count)
    peers = row_count // CORES
    message = (capacity * panels + TAIL, width)
    vmem = pl.BlockSpec(memory_space=pltpu.VMEM)
    smem = pl.BlockSpec(memory_space=pltpu.SMEM)
    hbm = pl.BlockSpec(memory_space=pl.ANY)
    dma = pltpu.SemaphoreType.DMA

    messages = row_count * col_count
    got, ids = pl.pallas_call(
        functools.partial(exchange_kernel, row_count, col_count, capacity),
        out_shape=(
            jax.ShapeDtypeStruct((row_count, col_count) + message, jnp.bfloat16),
            jax.ShapeDtypeStruct((messages, width), jnp.int32),
        ),
        in_specs=[smem, smem, hbm, hbm],
        out_specs=(hbm, vmem),
        scratch_shapes=[
            pltpu.VMEM((entries, 2 * panels, depth), jnp.bfloat16),
            pltpu.VMEM(shell_velocity.shape, jnp.bfloat16),
            pltpu.VMEM((col_count,) + message, jnp.bfloat16),
            pltpu.VMEM((row_count, col_count, TAIL, width), jnp.bfloat16),
            dma((2,)),
            dma((1,)),
            dma((col_count,)),
            dma((peers, col_count)),
            dma((peers, col_count)),
            dma((row_count, col_count)),
        ],
        compiler_params=pltpu.CompilerParams(
            collective_id=0, has_side_effects=True, vmem_limit_bytes=56 * 1024 * 1024
        ),
        name="exchange",
    )(
        coupling_dest,
        coupling_cluster,
        coupling.reshape(entries, 2 * panels, depth),
        shell_velocity,
    )

    got = got.reshape((messages,) + message)
    near_count, far_count, rank = near_blocks.shape[2], far_v.shape[2], far_v.shape[4]
    near = near_blocks.reshape(near_count, 2 * panels, panels)
    right = far_v.reshape(far_count, 2 * rank, panels)
    left = far_u.reshape(far_count, 2 * rank, panels)
    steps = 8
    partial_rows = pl.pallas_call(
        functools.partial(field_kernel, steps, capacity),
        grid=(steps,),
        out_shape=jax.ShapeDtypeStruct((RC_DEV, panels, width), jnp.bfloat16),
        in_specs=[
            smem,
            smem,
            vmem,
            pl.BlockSpec((near_count // steps, 2 * panels, panels), lambda i: (i, 0, 0)),
            pl.BlockSpec((far_count // steps, 2 * rank, panels), lambda i: (i, 0, 0)),
            pl.BlockSpec((far_count // steps, 2 * rank, panels), lambda i: (i, 0, 0)),
        ],
        out_specs=pl.BlockSpec((RC_DEV, panels, width), lambda i: (0, 0, 0)),
        scratch_shapes=[
            pltpu.SMEM((CC_DEV,), jnp.int32),
            pltpu.SMEM((messages * capacity,), jnp.int32),
            pltpu.VMEM((CC_DEV, panels, width), jnp.bfloat16),
            pltpu.VMEM((RC_DEV, 2 * panels, width), jnp.float32),
            pltpu.VMEM((RC_DEV, panels, width), jnp.float32),
        ],
        compiler_params=pltpu.CompilerParams(vmem_limit_bytes=56 * 1024 * 1024),
        name="fields",
    )(ids, block_pairs.reshape(-1), got, near, right, left)

    out_rows = RC_DEV * panels // col_count
    xs = 1
    while 4 * xs * xs <= col_count:
        xs *= 2
    zs = col_count // xs
    return pl.pallas_call(
        functools.partial(reduce_kernel, zs, xs),
        out_shape=jax.ShapeDtypeStruct((out_rows, width), jnp.bfloat16),
        in_specs=[hbm],
        out_specs=vmem,
        scratch_shapes=[
            pltpu.VMEM((zs, out_rows, width), jnp.bfloat16),
            pltpu.VMEM((zs, xs, out_rows, width), jnp.bfloat16),
            pltpu.VMEM((zs, out_rows, width), jnp.bfloat16),
            pltpu.VMEM((zs, out_rows, width), jnp.bfloat16),
            dma((zs,)),
            dma((zs, xs)),
            dma((zs, xs)),
            dma((zs,)),
            dma((zs,)),
        ],
        compiler_params=pltpu.CompilerParams(
            collective_id=1, has_side_effects=True, vmem_limit_bytes=56 * 1024 * 1024
        ),
        name="reduce",
    )(partial_rows.reshape(col_count, out_rows, width))


def solution(mesh):
    return jax.shard_map(
        functools.partial(per_device, mesh.shape["row"], mesh.shape["col"]),
        mesh=mesh,
        in_specs=(
            P(("row", "col"), None, None),
            P(("row", "col"), None, None, None, None),
            P(("row", "col"), None),
            P(("row", "col"), None),
            P("row", "col", None, None, None, None),
            P("row", "col", None, None, None, None),
            P("row", "col", None, None, None, None),
            P("row", "col", None),
        ),
        out_specs=P(("row", "col"), None),
        check_vma=False,
    )
```

```python
import functools

import jax
import jax.numpy as jnp
from jax import lax
from jax.experimental import pallas as pl
from jax.experimental.pallas import tpu as pltpu
from jax.sharding import PartitionSpec as P

RC_DEV = 16
CC_DEV = 64
NEAR_DEV = 32
CORES = 2
PIECES = 2
TAIL = 16
MESH = pl.DeviceIdType.MESH


def rotate(values):
    half = values.shape[-1] // 2
    lane = lax.broadcasted_iota(jnp.int32, values.shape, values.ndim - 1)
    turned = pltpu.roll(values, half, values.ndim - 1)
    return jnp.where(lane < half, -turned, turned)


def flip(index, mask, size):
    result, bit = 0, 1
    while bit < size:
        result = result + bit * ((index // bit + mask // bit) % 2)
        bit *= 2
    return result


def exchange_kernel(
    rows, cols, capacity, dest_ref, cluster_ref, coupling_hbm, velocity_hbm, got_ref, ids_ref,
    coupling_ref, velocity_ref, outgoing, tails, load_sem, tail_sem, send_col, send_y,
    send_core, recv,
):
    g, h = lax.axis_index("row"), lax.axis_index("col")
    entries, twice, _ = coupling_ref.shape
    panels = twice // 2
    width = velocity_ref.shape[-1]
    top = entries // velocity_ref.shape[0]
    peers = rows // CORES
    y, core = g // CORES, g % CORES
    mate = y * CORES + (CORES - 1 - core)

    loads = (
        pltpu.make_async_copy(coupling_hbm, coupling_ref, load_sem.at[0]),
        pltpu.make_async_copy(velocity_hbm, velocity_ref, load_sem.at[1]),
    )
    for load in loads:
        load.start()

    barrier = pltpu.get_barrier_semaphore()
    for step in range(1, cols):
        pl.semaphore_signal(barrier, inc=1, device_id=(g, (h + step) % cols), device_id_type=MESH)
    for step in range(1, peers):
        pl.semaphore_signal(
            barrier, inc=1, device_id=((y + step) % peers * CORES + core, h), device_id_type=MESH
        )
    pl.semaphore_signal(barrier, inc=1, device_id=(mate, h), device_id_type=MESH)
    for load in loads:
        load.wait()

    def rows_of(k):
        return pl.ds(0, TAIL + panels) if k == 0 else pl.ds(TAIL + k * panels, panels)

    def fill(j, send):
        target = flip(h, j, cols)
        picked = [jnp.int32(-1)] * capacity
        count = jnp.int32(0)
        for e in range(entries):
            hit = dest_ref[e % top, e // top] == target
            for k in range(capacity):
                picked[k] = jnp.where(hit & (count == k), e, picked[k])
            count = count + jnp.where(hit, 1, 0)
        lane = lax.broadcasted_iota(jnp.int32, (TAIL, width), 1)
        tail = jnp.zeros((TAIL, width), jnp.float32)
        for k in range(capacity):
            e = jnp.maximum(picked[k], 0)
            number = jnp.where(picked[k] >= 0, cluster_ref[e % top, e // top], 0)
            tail = jnp.where(lane == k, number.astype(jnp.float32), tail)
        outgoing[j, pl.ds(0, TAIL), :] = tail.astype(jnp.bfloat16)
        for k in range(capacity):
            e = jnp.maximum(picked[k], 0)
            product = jnp.dot(
                coupling_ref[e], velocity_ref[e // top], preferred_element_type=jnp.float32
            )
            value = product[:panels] + rotate(product[panels:])
            scale = jnp.where(picked[k] >= 0, 1.0, 0.0)
            outgoing[j, pl.ds(TAIL + k * panels, panels), :] = (value * scale).astype(jnp.bfloat16)
            send(k)

    def col_copy(j, k):
        target = flip(h, j, cols)
        return pltpu.make_async_remote_copy(
            src_ref=outgoing.at[j, rows_of(k), :],
            dst_ref=got_ref.at[g, h, rows_of(k), :],
            send_sem=send_col.at[j, k],
            recv_sem=recv.at[g, h, k],
            device_id=(g, target),
            device_id_type=MESH,
        )

    def relay_copy(origin, source, k, own, send_sem, row):
        block = outgoing.at[0, rows_of(k), :] if own else got_ref.at[origin, source, rows_of(k), :]
        return pltpu.make_async_remote_copy(
            src_ref=block,
            dst_ref=got_ref.at[origin, source, rows_of(k), :],
            send_sem=send_sem,
            recv_sem=recv.at[origin, source, k],
            device_id=(row, h),
            device_id_type=MESH,
        )

    def y_copy(step, j, k, own=False):
        source = flip(h, j, cols)
        row = (y + step) % peers * CORES + core
        return relay_copy(g, source, k, own, send_y.at[step, j, k], row)

    def core_copy(step, j, k, own=False):
        source = flip(h, j, cols)
        origin = (y + step) % peers * CORES + core
        return relay_copy(origin, source, k, own, send_core.at[step, j, k], mate)

    def arrived(origin, j, k):
        block = got_ref.at[origin, flip(h, j, cols), rows_of(k), :]
        pltpu.make_async_copy(block, block, recv.at[origin, flip(h, j, cols), k]).wait()

    def hand_out(k):
        for step in range(1, peers):
            y_copy(step, 0, k, True).start()
        core_copy(0, 0, k, True).start()

    fill(0, lambda k: None)
    own = pltpu.make_async_copy(outgoing.at[0], got_ref.at[g, h], tail_sem.at[0])
    own.start()
    pl.semaphore_wait(barrier, cols - 1 + peers - 1 + 1)
    for k in range(capacity):
        hand_out(k)

    @pl.loop(1, cols)
    def _(j):
        fill(j, lambda k: col_copy(j, k).start())

    lag = cols // 2

    def pass_on(j):
        for k in range(capacity):
            arrived(g, j, k)
            for step in range(1, peers):
                y_copy(step, j, k).start()
            core_copy(0, j, k).start()

    def relay(j):
        for k in range(capacity):
            for step in range(1, peers):
                arrived((y + step) % peers * CORES + core, j, k)
                core_copy(step, j, k).start()

    @pl.loop(1, lag)
    def _(j):
        pass_on(j)

    @pl.loop(lag, cols)
    def _(j):
        pass_on(j)
        relay(j - lag)

    @pl.loop(cols - lag, cols)
    def _(j):
        relay(j)

    @pl.loop(0, cols)
    def _(j):
        for step in range(peers):
            for k in range(capacity):
                arrived((y + step) % peers * CORES + (CORES - 1 - core), j, k)

    own.wait()
    gather = pltpu.make_async_copy(
        got_ref.at[:, :, pl.ds(0, TAIL), :], tails, tail_sem.at[1]
    )
    gather.start()
    gather.wait()
    for q in range(rows * cols):
        row = tails[q // cols, q % cols].astype(jnp.float32)
        ids_ref[pl.ds(q, 1), :] = row[:1].astype(jnp.int32)

    @pl.loop(1, cols)
    def _(j):
        for k in range(capacity):
            col_copy(j, k).wait_send()

    for k in range(capacity):
        for step in range(1, peers):
            y_copy(step, 0, k, True).wait_send()
            core_copy(step, 0, k).wait_send()
        core_copy(0, 0, k, True).wait_send()

    @pl.loop(1, cols)
    def _(j):
        for k in range(capacity):
            for step in range(1, peers):
                y_copy(step, j, k).wait_send()
            for step in range(peers):
                core_copy(step, j, k).wait_send()


def field_kernel(
    steps, capacity, ids_ref, pairs_ref, got_ref, near_ref, v_ref, u_ref, out_ref,
    head, link, sources, near_total, far_total,
):
    step = pl.program_id(0)
    messages, _, width = got_ref.shape
    near_count, twice, panels = near_ref.shape
    far_count, rank2, _ = v_ref.shape
    rank = rank2 // 2

    @pl.when(step == 0)
    def _():
        @pl.loop(0, CC_DEV)
        def _(c):
            head[c] = -1

        @pl.loop(0, messages)
        def _(q):
            for k in range(capacity):
                c = ids_ref[q, k]
                link[q * capacity + k] = head[c]
                head[c] = q * capacity + k

        @pl.loop(0, CC_DEV)
        def _(c):
            def more(state):
                return state[0] >= 0

            def add(state):
                n, value = state
                start = pl.multiple_of(TAIL + n % capacity * panels, TAIL)
                block = got_ref[n // capacity, pl.ds(start, panels), :]
                return link[n], value + block.astype(jnp.float32)

            _, value = lax.while_loop(
                more, add, (head[c], jnp.zeros((panels, width), jnp.float32))
            )
            sources[c] = value.astype(jnp.bfloat16)

        near_total[...] = jnp.zeros_like(near_total)
        far_total[...] = jnp.zeros_like(far_total)

    codes = [pairs_ref[steps * near_count + step * far_count + b] for b in range(far_count)]
    parts = [
        jnp.dot(v_ref[b], sources[codes[b] % CC_DEV], preferred_element_type=jnp.float32)
        for b in range(far_count)
    ]
    boths = []
    for part in parts:
        coeffs = part[:rank] + rotate(part[rank:])
        boths.append(jnp.concatenate([coeffs, rotate(coeffs)], axis=0).astype(jnp.bfloat16))

    for b in range(near_count):
        code = pairs_ref[step * near_count + b]
        near_total[code // CC_DEV] += jnp.dot(
            near_ref[b], sources[code % CC_DEV], preferred_element_type=jnp.float32
        )

    for b in range(far_count):
        far_total[codes[b] // CC_DEV] += lax.dot_general(
            u_ref[b], boths[b], (((0,), (0,)), ((), ())), preferred_element_type=jnp.float32
        )

    @pl.when(step == steps - 1)
    def _():
        @pl.loop(0, RC_DEV)
        def _(r):
            value = near_total[r, pl.ds(0, panels), :] + far_total[r]
            value = value + rotate(near_total[r, pl.ds(panels, panels), :])
            out_ref[r] = value.astype(jnp.bfloat16)


def reduce_kernel(
    zs, xs, part_ref, out_ref, mine, first, middle, second, load_sem, send1, recv1, send2, recv2
):
    g, h = lax.axis_index("row"), lax.axis_index("col")
    z, x = h // xs, h % xs

    loads = [
        pltpu.make_async_copy(part_ref.at[goal * xs + x], mine.at[goal], load_sem.at[goal])
        for goal in range(zs)
    ]
    for load in loads:
        load.start()

    barrier = pltpu.get_barrier_semaphore()
    for d in range(1, xs):
        pl.semaphore_signal(
            barrier, inc=1, device_id=(g, z * xs + (x + d) % xs), device_id_type=MESH
        )
    for k in range(1, zs):
        pl.semaphore_signal(
            barrier, inc=1, device_id=(g, (z + k) % zs * xs + x), device_id_type=MESH
        )
    pl.semaphore_wait(barrier, xs - 1 + zs - 1)

    rows = out_ref.shape[0] // PIECES
    parts = [pl.ds(p * rows, rows) for p in range(PIECES)]

    def x_copy(k, d, p):
        goal, other = flip(z, k, zs), (x + d) % xs
        return pltpu.make_async_remote_copy(
            src_ref=part_ref.at[goal * xs + other, parts[p], :],
            dst_ref=first.at[goal, x, parts[p], :],
            send_sem=send1.at[goal, other, p],
            recv_sem=recv1.at[goal, x, p],
            device_id=(g, z * xs + other),
            device_id_type=MESH,
        )

    def z_copy(k, p):
        goal = flip(z, k, zs)
        return pltpu.make_async_remote_copy(
            src_ref=middle.at[goal, parts[p], :],
            dst_ref=second.at[z, parts[p], :],
            send_sem=send2.at[goal, p],
            recv_sem=recv2.at[z, p],
            device_id=(g, goal * xs + x),
            device_id_type=MESH,
        )

    order = [(k, p) for k in reversed(range(zs)) for p in range(PIECES)]
    for k, p in order:
        for d in range(1, xs):
            x_copy(k, d, p).start()
    for load in loads:
        load.wait()
    totals = [None] * PIECES
    for k, p in order:
        goal = flip(z, k, zs)
        value = mine[goal, parts[p], :].astype(jnp.float32)
        for d in range(1, xs):
            other = (x + d) % xs
            block = first.at[goal, other, parts[p], :]
            pltpu.make_async_copy(block, block, recv1.at[goal, other, p]).wait()
            value = value + first[goal, other, parts[p], :].astype(jnp.float32)
        if k:
            middle[goal, parts[p], :] = value.astype(jnp.bfloat16)
            z_copy(k, p).start()
        else:
            totals[p] = value
    for p in range(PIECES):
        value = totals[p]
        for k in range(1, zs):
            source = flip(z, k, zs)
            block = second.at[source, parts[p], :]
            pltpu.make_async_copy(block, block, recv2.at[source, p]).wait()
            value = value + second[source, parts[p], :].astype(jnp.float32)
        out_ref[parts[p], :] = value.astype(jnp.bfloat16)
    for k, p in order:
        for d in range(1, xs):
            x_copy(k, d, p).wait_send()
        if k:
            z_copy(k, p).wait_send()


def per_device(
    row_count, col_count,
    shell_velocity, coupling, coupling_dest, coupling_cluster, near_blocks, far_v, far_u,
    block_pairs,
):
    width = shell_velocity.shape[-1]
    shells, top, _, panels, depth = coupling.shape
    entries = shells * top
    capacity = max(2, (entries + col_count - 1) // col_count)
    peers = row_count // CORES
    message = (capacity * panels + TAIL, width)
    vmem = pl.BlockSpec(memory_space=pltpu.VMEM)
    smem = pl.BlockSpec(memory_space=pltpu.SMEM)
    hbm = pl.BlockSpec(memory_space=pl.ANY)
    dma = pltpu.SemaphoreType.DMA

    messages = row_count * col_count
    got, ids = pl.pallas_call(
        functools.partial(exchange_kernel, row_count, col_count, capacity),
        out_shape=(
            jax.ShapeDtypeStruct((row_count, col_count) + message, jnp.bfloat16),
            jax.ShapeDtypeStruct((messages, width), jnp.int32),
        ),
        in_specs=[smem, smem, hbm, hbm],
        out_specs=(hbm, vmem),
        scratch_shapes=[
            pltpu.VMEM((entries, 2 * panels, depth), jnp.bfloat16),
            pltpu.VMEM(shell_velocity.shape, jnp.bfloat16),
            pltpu.VMEM((col_count,) + message, jnp.bfloat16),
            pltpu.VMEM((row_count, col_count, TAIL, width), jnp.bfloat16),
            dma((2,)),
            dma((2,)),
            dma((col_count, capacity)),
            dma((peers, col_count, capacity)),
            dma((peers, col_count, capacity)),
            dma((row_count, col_count, capacity)),
        ],
        compiler_params=pltpu.CompilerParams(
            collective_id=0, has_side_effects=True, vmem_limit_bytes=56 * 1024 * 1024
        ),
        name="exchange",
    )(
        coupling_dest.T,
        coupling_cluster.T,
        coupling.reshape(entries, 2 * panels, depth),
        shell_velocity,
    )

    got = got.reshape((messages,) + message)
    near_count, far_count, rank = near_blocks.shape[2], far_v.shape[2], far_v.shape[4]
    near = near_blocks.reshape(near_count, 2 * panels, panels)
    right = far_v.reshape(far_count, 2 * rank, panels)
    left = far_u.reshape(far_count, 2 * rank, panels)
    steps = 8
    partial_rows = pl.pallas_call(
        functools.partial(field_kernel, steps, capacity),
        grid=(steps,),
        out_shape=jax.ShapeDtypeStruct((RC_DEV, panels, width), jnp.bfloat16),
        in_specs=[
            smem,
            smem,
            vmem,
            pl.BlockSpec((near_count // steps, 2 * panels, panels), lambda i: (i, 0, 0)),
            pl.BlockSpec((far_count // steps, 2 * rank, panels), lambda i: (i, 0, 0)),
            pl.BlockSpec((far_count // steps, 2 * rank, panels), lambda i: (i, 0, 0)),
        ],
        out_specs=pl.BlockSpec((RC_DEV, panels, width), lambda i: (0, 0, 0)),
        scratch_shapes=[
            pltpu.SMEM((CC_DEV,), jnp.int32),
            pltpu.SMEM((messages * capacity,), jnp.int32),
            pltpu.VMEM((CC_DEV, panels, width), jnp.bfloat16),
            pltpu.VMEM((RC_DEV, 2 * panels, width), jnp.float32),
            pltpu.VMEM((RC_DEV, panels, width), jnp.float32),
        ],
        compiler_params=pltpu.CompilerParams(vmem_limit_bytes=56 * 1024 * 1024),
        name="fields",
    )(ids, block_pairs.reshape(-1), got, near, right, left)

    out_rows = RC_DEV * panels // col_count
    xs = 1
    while 4 * xs * xs <= col_count:
        xs *= 2
    zs = col_count // xs
    return pl.pallas_call(
        functools.partial(reduce_kernel, zs, xs),
        out_shape=jax.ShapeDtypeStruct((out_rows, width), jnp.bfloat16),
        in_specs=[pl.BlockSpec(memory_space=pltpu.HBM)],
        out_specs=vmem,
        scratch_shapes=[
            pltpu.VMEM((zs, out_rows, width), jnp.bfloat16),
            pltpu.VMEM((zs, xs, out_rows, width), jnp.bfloat16),
            pltpu.VMEM((zs, out_rows, width), jnp.bfloat16),
            pltpu.VMEM((zs, out_rows, width), jnp.bfloat16),
            dma((zs,)),
            dma((zs, xs, PIECES)),
            dma((zs, xs, PIECES)),
            dma((zs, PIECES)),
            dma((zs, PIECES)),
        ],
        compiler_params=pltpu.CompilerParams(
            collective_id=1, has_side_effects=True, vmem_limit_bytes=56 * 1024 * 1024
        ),
        name="reduce",
    )(partial_rows.reshape(col_count, out_rows, width))


def solution(mesh):
    return jax.shard_map(
        functools.partial(per_device, mesh.shape["row"], mesh.shape["col"]),
        mesh=mesh,
        in_specs=(
            P(("row", "col"), None, None),
            P(("row", "col"), None, None, None, None),
            P(("row", "col"), None),
            P(("row", "col"), None),
            P("row", "col", None, None, None, None),
            P("row", "col", None, None, None, None),
            P("row", "col", None, None, None, None),
            P("row", "col", None),
        ),
        out_specs=P(("row", "col"), None),
        check_vma=False,
    )
```

```python
import functools

import jax
import jax.numpy as jnp
from jax import lax
from jax.experimental import pallas as pl
from jax.experimental.pallas import tpu as pltpu
from jax.sharding import PartitionSpec as P

RC_DEV = 16
CC_DEV = 64
NEAR_DEV = 32
CORES = 2
PIECES = 4
TAIL = 16
MESH = pl.DeviceIdType.MESH


def rotate(values):
    half = values.shape[-1] // 2
    lane = lax.broadcasted_iota(jnp.int32, values.shape, values.ndim - 1)
    turned = pltpu.roll(values, half, values.ndim - 1)
    return jnp.where(lane < half, -turned, turned)


def flip(index, mask, size):
    result, bit = 0, 1
    while bit < size:
        result = result + bit * ((index // bit + mask // bit) % 2)
        bit *= 2
    return result


def exchange_kernel(
    rows, cols, capacity, dest_ref, cluster_ref, coupling_hbm, velocity_hbm, got_ref, ids_ref,
    coupling_ref, velocity_ref, outgoing, tails, load_sem, tail_sem, send_col, send_y,
    send_core, recv,
):
    g, h = lax.axis_index("row"), lax.axis_index("col")
    entries, twice, _ = coupling_ref.shape
    panels = twice // 2
    width = velocity_ref.shape[-1]
    top = entries // velocity_ref.shape[0]
    peers = rows // CORES
    y, core = g // CORES, g % CORES
    mate = y * CORES + (CORES - 1 - core)

    loads = (
        pltpu.make_async_copy(coupling_hbm, coupling_ref, load_sem.at[0]),
        pltpu.make_async_copy(velocity_hbm, velocity_ref, load_sem.at[1]),
    )
    for load in loads:
        load.start()

    barrier = pltpu.get_barrier_semaphore()
    for step in range(1, cols):
        pl.semaphore_signal(barrier, inc=1, device_id=(g, (h + step) % cols), device_id_type=MESH)
    for step in range(1, peers):
        pl.semaphore_signal(
            barrier, inc=1, device_id=((y + step) % peers * CORES + core, h), device_id_type=MESH
        )
    pl.semaphore_signal(barrier, inc=1, device_id=(mate, h), device_id_type=MESH)
    for load in loads:
        load.wait()

    def rows_of(k):
        return pl.ds(0, TAIL + panels) if k == 0 else pl.ds(TAIL + k * panels, panels)

    def fill(j, send):
        target = flip(h, j, cols)
        picked = [jnp.int32(-1)] * capacity
        count = jnp.int32(0)
        for e in range(entries):
            hit = dest_ref[e % top, e // top] == target
            for k in range(capacity):
                picked[k] = jnp.where(hit & (count == k), e, picked[k])
            count = count + jnp.where(hit, 1, 0)
        lane = lax.broadcasted_iota(jnp.int32, (TAIL, width), 1)
        tail = jnp.zeros((TAIL, width), jnp.float32)
        for k in range(capacity):
            e = jnp.maximum(picked[k], 0)
            number = jnp.where(picked[k] >= 0, cluster_ref[e % top, e // top], 0)
            tail = jnp.where(lane == k, number.astype(jnp.float32), tail)
        outgoing[j, pl.ds(0, TAIL), :] = tail.astype(jnp.bfloat16)
        for k in range(capacity):
            e = jnp.maximum(picked[k], 0)
            product = jnp.dot(
                coupling_ref[e], velocity_ref[e // top], preferred_element_type=jnp.float32
            )
            value = product[:panels] + rotate(product[panels:])
            scale = jnp.where(picked[k] >= 0, 1.0, 0.0)
            outgoing[j, pl.ds(TAIL + k * panels, panels), :] = (value * scale).astype(jnp.bfloat16)
            send(k)

    def col_copy(j, k):
        target = flip(h, j, cols)
        return pltpu.make_async_remote_copy(
            src_ref=outgoing.at[j, rows_of(k), :],
            dst_ref=got_ref.at[g, h, rows_of(k), :],
            send_sem=send_col.at[j, k],
            recv_sem=recv.at[g, h, k],
            device_id=(g, target),
            device_id_type=MESH,
        )

    def relay_copy(origin, source, k, own, send_sem, row):
        block = outgoing.at[0, rows_of(k), :] if own else got_ref.at[origin, source, rows_of(k), :]
        return pltpu.make_async_remote_copy(
            src_ref=block,
            dst_ref=got_ref.at[origin, source, rows_of(k), :],
            send_sem=send_sem,
            recv_sem=recv.at[origin, source, k],
            device_id=(row, h),
            device_id_type=MESH,
        )

    def y_copy(step, j, k, own=False):
        source = flip(h, j, cols)
        row = (y + step) % peers * CORES + core
        return relay_copy(g, source, k, own, send_y.at[step, j, k], row)

    def core_copy(step, j, k, own=False):
        source = flip(h, j, cols)
        origin = (y + step) % peers * CORES + core
        return relay_copy(origin, source, k, own, send_core.at[step, j, k], mate)

    def arrived(origin, j, k):
        block = got_ref.at[origin, flip(h, j, cols), rows_of(k), :]
        pltpu.make_async_copy(block, block, recv.at[origin, flip(h, j, cols), k]).wait()

    def hand_out(k):
        for step in range(1, peers):
            y_copy(step, 0, k, True).start()
        core_copy(0, 0, k, True).start()

    fill(0, lambda k: None)
    own = pltpu.make_async_copy(outgoing.at[0], got_ref.at[g, h], tail_sem.at[0])
    own.start()
    pl.semaphore_wait(barrier, cols - 1 + peers - 1 + 1)
    for k in range(capacity):
        hand_out(k)

    @pl.loop(1, cols)
    def _(j):
        fill(j, lambda k: col_copy(j, k).start())

    lag = cols // 2

    def pass_on(j):
        for k in range(capacity):
            arrived(g, j, k)
            for step in range(1, peers):
                y_copy(step, j, k).start()
            core_copy(0, j, k).start()

    def relay(j):
        for k in range(capacity):
            for step in range(1, peers):
                arrived((y + step) % peers * CORES + core, j, k)
                core_copy(step, j, k).start()

    @pl.loop(1, lag)
    def _(j):
        pass_on(j)

    @pl.loop(lag, cols)
    def _(j):
        pass_on(j)
        relay(j - lag)

    @pl.loop(cols - lag, cols)
    def _(j):
        relay(j)

    @pl.loop(0, cols)
    def _(j):
        for step in range(peers):
            for k in range(capacity):
                arrived((y + step) % peers * CORES + (CORES - 1 - core), j, k)

    own.wait()
    gather = pltpu.make_async_copy(
        got_ref.at[:, :, pl.ds(0, TAIL), :], tails, tail_sem.at[1]
    )
    gather.start()
    gather.wait()
    for q in range(rows * cols):
        row = tails[q // cols, q % cols].astype(jnp.float32)
        ids_ref[pl.ds(q, 1), :] = row[:1].astype(jnp.int32)

    @pl.loop(1, cols)
    def _(j):
        for k in range(capacity):
            col_copy(j, k).wait_send()

    for k in range(capacity):
        for step in range(1, peers):
            y_copy(step, 0, k, True).wait_send()
            core_copy(step, 0, k).wait_send()
        core_copy(0, 0, k, True).wait_send()

    @pl.loop(1, cols)
    def _(j):
        for k in range(capacity):
            for step in range(1, peers):
                y_copy(step, j, k).wait_send()
            for step in range(peers):
                core_copy(step, j, k).wait_send()


def field_kernel(
    steps, capacity, ids_ref, pairs_ref, got_ref, near_ref, v_ref, u_ref, out_ref,
    head, link, sources, near_total, far_total,
):
    step = pl.program_id(0)
    messages, _, width = got_ref.shape
    near_count, twice, panels = near_ref.shape
    far_count, rank2, _ = v_ref.shape
    rank = rank2 // 2

    @pl.when(step == 0)
    def _():
        @pl.loop(0, CC_DEV)
        def _(c):
            head[c] = -1

        @pl.loop(0, messages)
        def _(q):
            for k in range(capacity):
                c = ids_ref[q, k]
                link[q * capacity + k] = head[c]
                head[c] = q * capacity + k

        @pl.loop(0, CC_DEV)
        def _(c):
            def block(n):
                start = pl.multiple_of(TAIL + n % capacity * panels, TAIL)
                return got_ref[n // capacity, pl.ds(start, panels), :]

            one = head[c]
            two = jnp.where(one >= 0, link[jnp.maximum(one, 0)], -1)
            three = jnp.where(two >= 0, link[jnp.maximum(two, 0)], -1)

            @pl.when(one < 0)
            def _():
                sources[c] = jnp.zeros((panels, width), jnp.bfloat16)

            @pl.when((one >= 0) & (two < 0))
            def _():
                sources[c] = block(one)

            @pl.when((two >= 0) & (three < 0))
            def _():
                value = block(one).astype(jnp.float32) + block(two).astype(jnp.float32)
                sources[c] = value.astype(jnp.bfloat16)

            @pl.when(three >= 0)
            def _():
                def add(state):
                    n, value = state
                    return link[n], value + block(n).astype(jnp.float32)

                value = block(one).astype(jnp.float32) + block(two).astype(jnp.float32)
                _, value = lax.while_loop(lambda state: state[0] >= 0, add, (three, value))
                sources[c] = value.astype(jnp.bfloat16)

        near_total[...] = jnp.zeros_like(near_total)
        far_total[...] = jnp.zeros_like(far_total)

    codes = [pairs_ref[steps * near_count + step * far_count + b] for b in range(far_count)]
    parts = [
        jnp.dot(v_ref[b], sources[codes[b] % CC_DEV], preferred_element_type=jnp.float32)
        for b in range(far_count)
    ]
    boths = []
    for part in parts:
        coeffs = part[:rank] + rotate(part[rank:])
        boths.append(jnp.concatenate([coeffs, rotate(coeffs)], axis=0).astype(jnp.bfloat16))

    for b in range(near_count):
        code = pairs_ref[step * near_count + b]
        near_total[code // CC_DEV] += jnp.dot(
            near_ref[b], sources[code % CC_DEV], preferred_element_type=jnp.float32
        )

    for b in range(far_count):
        far_total[codes[b] // CC_DEV] += lax.dot_general(
            u_ref[b], boths[b], (((0,), (0,)), ((), ())), preferred_element_type=jnp.float32
        )

    @pl.when(step == steps - 1)
    def _():
        @pl.loop(0, RC_DEV)
        def _(r):
            value = near_total[r, pl.ds(0, panels), :] + far_total[r]
            value = value + rotate(near_total[r, pl.ds(panels, panels), :])
            out_ref[r] = value.astype(jnp.bfloat16)


def reduce_kernel(
    zs, xs, part_ref, out_ref, mine, first, middle, second, load_sem, send1, recv1, send2, recv2
):
    g, h = lax.axis_index("row"), lax.axis_index("col")
    z, x = h // xs, h % xs

    loads = [
        pltpu.make_async_copy(part_ref.at[goal * xs + x], mine.at[goal], load_sem.at[goal])
        for goal in range(zs)
    ]
    for load in loads:
        load.start()

    barrier = pltpu.get_barrier_semaphore()
    for d in range(1, xs):
        pl.semaphore_signal(
            barrier, inc=1, device_id=(g, z * xs + (x + d) % xs), device_id_type=MESH
        )
    for k in range(1, zs):
        pl.semaphore_signal(
            barrier, inc=1, device_id=(g, (z + k) % zs * xs + x), device_id_type=MESH
        )
    pl.semaphore_wait(barrier, xs - 1 + zs - 1)

    rows = out_ref.shape[0] // PIECES
    parts = [pl.ds(p * rows, rows) for p in range(PIECES)]

    def x_copy(k, d, p):
        goal, other = flip(z, k, zs), (x + d) % xs
        return pltpu.make_async_remote_copy(
            src_ref=part_ref.at[goal * xs + other, parts[p], :],
            dst_ref=first.at[goal, x, parts[p], :],
            send_sem=send1.at[goal, other, p],
            recv_sem=recv1.at[goal, x, p],
            device_id=(g, z * xs + other),
            device_id_type=MESH,
        )

    def z_copy(k, p):
        goal = flip(z, k, zs)
        return pltpu.make_async_remote_copy(
            src_ref=middle.at[goal, parts[p], :],
            dst_ref=second.at[z, parts[p], :],
            send_sem=send2.at[goal, p],
            recv_sem=recv2.at[z, p],
            device_id=(g, goal * xs + x),
            device_id_type=MESH,
        )

    order = [(k, p) for k in reversed(range(zs)) for p in range(PIECES)]
    for k, p in order:
        for d in range(1, xs):
            x_copy(k, d, p).start()
    for load in loads:
        load.wait()
    totals = [None] * PIECES
    for k, p in order:
        goal = flip(z, k, zs)
        value = mine[goal, parts[p], :].astype(jnp.float32)
        for d in range(1, xs):
            other = (x + d) % xs
            block = first.at[goal, other, parts[p], :]
            pltpu.make_async_copy(block, block, recv1.at[goal, other, p]).wait()
            value = value + first[goal, other, parts[p], :].astype(jnp.float32)
        if k:
            middle[goal, parts[p], :] = value.astype(jnp.bfloat16)
            z_copy(k, p).start()
        else:
            totals[p] = value
    for p in range(PIECES):
        value = totals[p]
        for k in range(1, zs):
            source = flip(z, k, zs)
            block = second.at[source, parts[p], :]
            pltpu.make_async_copy(block, block, recv2.at[source, p]).wait()
            value = value + second[source, parts[p], :].astype(jnp.float32)
        out_ref[parts[p], :] = value.astype(jnp.bfloat16)
    for k, p in order:
        for d in range(1, xs):
            x_copy(k, d, p).wait_send()
        if k:
            z_copy(k, p).wait_send()


def per_device(
    row_count, col_count,
    shell_velocity, coupling, coupling_dest, coupling_cluster, near_blocks, far_v, far_u,
    block_pairs,
):
    width = shell_velocity.shape[-1]
    shells, top, _, panels, depth = coupling.shape
    entries = shells * top
    capacity = max(2, (entries + col_count - 1) // col_count)
    peers = row_count // CORES
    message = (capacity * panels + TAIL, width)
    vmem = pl.BlockSpec(memory_space=pltpu.VMEM)
    smem = pl.BlockSpec(memory_space=pltpu.SMEM)
    hbm = pl.BlockSpec(memory_space=pl.ANY)
    dma = pltpu.SemaphoreType.DMA

    messages = row_count * col_count
    got, ids = pl.pallas_call(
        functools.partial(exchange_kernel, row_count, col_count, capacity),
        out_shape=(
            jax.ShapeDtypeStruct((row_count, col_count) + message, jnp.bfloat16),
            jax.ShapeDtypeStruct((messages, width), jnp.int32),
        ),
        in_specs=[smem, smem, hbm, hbm],
        out_specs=(hbm, vmem),
        scratch_shapes=[
            pltpu.VMEM((entries, 2 * panels, depth), jnp.bfloat16),
            pltpu.VMEM(shell_velocity.shape, jnp.bfloat16),
            pltpu.VMEM((col_count,) + message, jnp.bfloat16),
            pltpu.VMEM((row_count, col_count, TAIL, width), jnp.bfloat16),
            dma((2,)),
            dma((2,)),
            dma((col_count, capacity)),
            dma((peers, col_count, capacity)),
            dma((peers, col_count, capacity)),
            dma((row_count, col_count, capacity)),
        ],
        compiler_params=pltpu.CompilerParams(
            collective_id=0, has_side_effects=True, vmem_limit_bytes=56 * 1024 * 1024
        ),
        name="exchange",
    )(
        coupling_dest.T,
        coupling_cluster.T,
        coupling.reshape(entries, 2 * panels, depth),
        shell_velocity,
    )

    got = got.reshape((messages,) + message)
    near_count, far_count, rank = near_blocks.shape[2], far_v.shape[2], far_v.shape[4]
    near = near_blocks.reshape(near_count, 2 * panels, panels)
    right = far_v.reshape(far_count, 2 * rank, panels)
    left = far_u.reshape(far_count, 2 * rank, panels)
    steps = 8
    partial_rows = pl.pallas_call(
        functools.partial(field_kernel, steps, capacity),
        grid=(steps,),
        out_shape=jax.ShapeDtypeStruct((RC_DEV, panels, width), jnp.bfloat16),
        in_specs=[
            smem,
            smem,
            vmem,
            pl.BlockSpec((near_count // steps, 2 * panels, panels), lambda i: (i, 0, 0)),
            pl.BlockSpec((far_count // steps, 2 * rank, panels), lambda i: (i, 0, 0)),
            pl.BlockSpec((far_count // steps, 2 * rank, panels), lambda i: (i, 0, 0)),
        ],
        out_specs=pl.BlockSpec((RC_DEV, panels, width), lambda i: (0, 0, 0)),
        scratch_shapes=[
            pltpu.SMEM((CC_DEV,), jnp.int32),
            pltpu.SMEM((messages * capacity,), jnp.int32),
            pltpu.VMEM((CC_DEV, panels, width), jnp.bfloat16),
            pltpu.VMEM((RC_DEV, 2 * panels, width), jnp.float32),
            pltpu.VMEM((RC_DEV, panels, width), jnp.float32),
        ],
        compiler_params=pltpu.CompilerParams(vmem_limit_bytes=56 * 1024 * 1024),
        name="fields",
    )(ids, block_pairs.reshape(-1), got, near, right, left)

    out_rows = RC_DEV * panels // col_count
    xs = 1
    while 4 * xs * xs <= col_count:
        xs *= 2
    zs = col_count // xs
    return pl.pallas_call(
        functools.partial(reduce_kernel, zs, xs),
        out_shape=jax.ShapeDtypeStruct((out_rows, width), jnp.bfloat16),
        in_specs=[pl.BlockSpec(memory_space=pltpu.HBM)],
        out_specs=vmem,
        scratch_shapes=[
            pltpu.VMEM((zs, out_rows, width), jnp.bfloat16),
            pltpu.VMEM((zs, xs, out_rows, width), jnp.bfloat16),
            pltpu.VMEM((zs, out_rows, width), jnp.bfloat16),
            pltpu.VMEM((zs, out_rows, width), jnp.bfloat16),
            dma((zs,)),
            dma((zs, xs, PIECES)),
            dma((zs, xs, PIECES)),
            dma((zs, PIECES)),
            dma((zs, PIECES)),
        ],
        compiler_params=pltpu.CompilerParams(
            collective_id=1, has_side_effects=True, vmem_limit_bytes=56 * 1024 * 1024
        ),
        name="reduce",
    )(partial_rows.reshape(col_count, out_rows, width))


def solution(mesh):
    return jax.shard_map(
        functools.partial(per_device, mesh.shape["row"], mesh.shape["col"]),
        mesh=mesh,
        in_specs=(
            P(("row", "col"), None, None),
            P(("row", "col"), None, None, None, None),
            P(("row", "col"), None),
            P(("row", "col"), None),
            P("row", "col", None, None, None, None),
            P("row", "col", None, None, None, None),
            P("row", "col", None, None, None, None),
            P("row", "col", None),
        ),
        out_specs=P(("row", "col"), None),
        check_vma=False,
    )
```
